512 devices in a mesh: replica: 32 (over z, x), tensor: 16 (over y, core).
Axes of the slice: x: 4, y: 8, z: 8, core: 2. Of those that a mesh axis runs over, the one named last changes fastest.
Arguments:
- hidden_acts: bfloat16 [16384, 16384], P('replica', 'tensor'), may hold values from -6 to 6
- out_grad: bfloat16 [16384, 768], P('replica'), may hold values from -0.25 to 0.25
- error_prev: bfloat16 [32, 768, 16384], P('replica', None, 'tensor'), may hold values from -6 to 6
- right_prev: bfloat16 [16384, 128], P('tensor'), may hold values from -6 to 6
Outputs:
- error_next: bfloat16 [32, 768, 16384], P('replica', None, 'tensor')
- right_next: float32 [16384, 128], P('tensor')
The draws below stay inside these ranges and needn't reach their ends.
All inputs are finite; a program needn't handle non-finite values.
Results may differ from the reference program's by a relative error of at most 0.0058.
Values may be sent and summed in bfloat16 or wider, within the bound.
No kernel may reach another device: no remote copies, remote signals or barrier semaphores. Data moves between devices by JAX's collectives and lax.ppermute only.
A program may use at most 64 MiB of HBM per device.

```python
import jax
import jax.numpy as jnp
from jax import lax

D = 768
FF = 16384
RANK = 128
TOK_DEV = 512
TOKENS = 16384
N_REPLICA = 32


def shard_levels(own_key, shape, split, least, largest):
    def one(axis_at, parts):
        heights = jax.random.uniform(jax.random.fold_in(jax.random.fold_in(own_key, 6), axis_at), (parts,), jnp.float32, least / len(split), largest / len(split))
        return jnp.repeat(jnp.exp(heights), shape[axis_at] // parts).reshape((-1,) + (1,) * (len(shape) - axis_at - 1))

    loudness = one(*split[0])
    for cut in split[1:]:
        loudness = loudness * one(*cut)
    return loudness


def noise(stream_key, extent, scale, limit, split=(), dtype=jnp.bfloat16):
    drawn = scale * jax.random.normal(stream_key, extent, jnp.float32)
    if split:
        drawn = drawn * shard_levels(stream_key, extent, split, -0.22, 0.18)
    return jnp.clip(drawn, -limit, limit).astype(dtype)


def setup_inputs(seed: int = 0) -> dict:
    arg_keys = jax.random.split(jax.random.key(seed), 5)
    hidden_acts = noise(arg_keys[0], (TOKENS, FF), 1.0, 6.0, ((0, 32), (1, 16)))
    out_grad = noise(arg_keys[1], (TOKENS, D), TOK_DEV ** -0.5, 0.25, ((0, 32),))
    error_prev = noise(arg_keys[2], (N_REPLICA, D, FF), 1.0, 6.0, ((0, 32), (2, 16)))
    right_prev = noise(arg_keys[3], (FF, RANK), 1.0, 6.0, ((0, 16),))
    return {"hidden_acts": hidden_acts, "out_grad": out_grad, "error_prev": error_prev, "right_prev": right_prev}


def compensate(acts, cot, err):
    grad = lax.dot_general(cot.astype(jnp.float32), acts.astype(jnp.float32), (((0,), (0,)), ((), ())), preferred_element_type=jnp.float32)
    return (grad + err.astype(jnp.float32)).astype(jnp.bfloat16)

def reference(hidden_acts, out_grad, error_prev, right_prev):
    acts = hidden_acts.reshape(N_REPLICA, TOK_DEV, FF)
    cots = out_grad.reshape(N_REPLICA, TOK_DEV, D)

    def left_term(carry, items):
        comp = compensate(items[0], items[1], items[2])
        return (carry + jnp.dot(comp.astype(jnp.float32), right_prev.astype(jnp.float32), preferred_element_type=jnp.float32), None)
    p_sum, unused = lax.scan(left_term, jnp.zeros((D, RANK), jnp.float32), (acts, cots, error_prev))
    gram_matrix = jnp.dot(p_sum.T, p_sum, precision=lax.Precision.HIGHEST)
    factor = jnp.linalg.cholesky(gram_matrix)
    left_low = jax.scipy.linalg.solve_triangular(factor, p_sum.T, lower=True).T.astype(jnp.bfloat16)

    def right_term(carry, items):
        comp = compensate(items[0], items[1], items[2])
        term = lax.dot_general(comp.astype(jnp.float32), left_low.astype(jnp.float32), (((0,), (0,)), ((), ())), preferred_element_type=jnp.float32)
        return (carry + term, None)
    right_total, unused = lax.scan(right_term, jnp.zeros((FF, RANK), jnp.float32), (acts, cots, error_prev))
    right_next = right_total / N_REPLICA
    right_low = right_next.astype(jnp.bfloat16)
    approx = lax.dot_general(left_low.astype(jnp.float32), right_low.astype(jnp.float32), (((1,), (1,)), ((), ())), preferred_element_type=jnp.float32)

    def new_error(items):
        comp = compensate(items[0], items[1], items[2])
        return (comp.astype(jnp.float32) - approx).astype(jnp.bfloat16)
    error_next = lax.map(new_error, (acts, cots, error_prev))
    return (error_next, right_next)
```

```python
import jax
import jax.numpy as jnp
from jax import lax
from jax.experimental import pallas as pl
from jax.experimental.pallas import tpu as pltpu
from jax.sharding import PartitionSpec as P

EXACT = lax.Precision.HIGHEST
SUB, LANE = 8, 128
PIVOTS = 8
PANEL = 64


def sum_at_owner(value, axis):
    parts = lax.axis_size(axis)
    blocks = value.reshape(parts, value.shape[0] // parts, value.shape[1])
    return lax.all_to_all(blocks, axis, split_axis=0, concat_axis=0, tiled=True)


def copy_for_each(value, axis):
    copies = jnp.broadcast_to(value, (lax.axis_size(axis), *value.shape))
    return lax.all_to_all(copies, axis, split_axis=0, concat_axis=0, tiled=True)


def collect(value, axis):
    return copy_for_each(value, axis).reshape(-1, value.shape[1])


def eliminate(gram, right, base):
    height, width = gram.shape
    groups = height // SUB
    gram = gram.reshape(groups, SUB, width)
    right = right.reshape(groups, SUB, width)
    shape = (groups, SUB, width)
    row_index = lax.broadcasted_iota(jnp.int32, shape, 0) * SUB + lax.broadcasted_iota(
        jnp.int32, shape, 1
    )

    def row(value, i):
        return jnp.broadcast_to(value[i // SUB, i % SUB : i % SUB + 1, :], (SUB, width))

    pivots = []
    for first in range(0, height, PIVOTS):
        columns = [
            jnp.broadcast_to(gram[:, :, base + first + k : base + first + k + 1], shape)
            for k in range(PIVOTS)
        ]
        corner = {
            (i, k): row(columns[k], first + i) for k in range(PIVOTS) for i in range(k + 1)
        }
        gram_rows = [row(gram, first + i) for i in range(PIVOTS)]
        right_rows = [row(right, first + i) for i in range(PIVOTS)]
        factors = []
        for i in range(PIVOTS):
            inverse = 1.0 / corner[i, i]
            pivots.append(corner[i, i][:1])
            for k in range(i + 1, PIVOTS):
                ratio = corner[i, k] * inverse
                for j in range(k, PIVOTS):
                    corner[k, j] = corner[k, j] - ratio * corner[i, j]
                columns[k] = columns[k] - columns[i] * ratio
                gram_rows[k] = gram_rows[k] - gram_rows[i] * ratio
                right_rows[k] = right_rows[k] - right_rows[i] * ratio
            factors.append(jnp.where(row_index > first + i, columns[i] * inverse, 0.0))
        for i in range(PIVOTS):
            gram = gram - factors[i] * gram_rows[i]
            right = right - factors[i] * right_rows[i]
    scale = lax.rsqrt(jnp.concatenate(pivots, axis=0))
    return gram.reshape(height, width) * scale, right.reshape(height, width) * scale


def orthonormal_body(p_ref, left_ref):
    p_sum = p_ref[...].astype(jnp.float32)
    gram = lax.dot_general(
        p_sum, p_sum, (((0,), (0,)), ((), ())), precision=EXACT, preferred_element_type=jnp.float32
    )
    rank = gram.shape[0]
    across = lax.broadcasted_iota(jnp.int32, (rank, rank), 0)
    along = lax.broadcasted_iota(jnp.int32, (rank, rank), 1)
    right = jnp.where(across == along, 1.0, 0.0)
    inverse = []
    for base in range(0, rank, PANEL):
        upper, done = eliminate(gram[:PANEL], right[:PANEL], base)
        inverse.append(done)
        if base + PANEL < rank:
            update = lax.dot_general(
                upper,
                jnp.concatenate([upper, done], axis=1),
                (((0,), (0,)), ((), ())),
                precision=EXACT,
                preferred_element_type=jnp.float32,
            )[base + PANEL :]
            gram = gram[PANEL:] - update[:, :rank]
            right = right[PANEL:] - update[:, rank:]
    left_ref[...] = lax.dot_general(
        p_sum,
        jnp.concatenate(inverse, axis=0),
        (((1,), (1,)), ((), ())),
        precision=EXACT,
        preferred_element_type=jnp.float32,
    ).astype(left_ref.dtype)


def orthonormal(p_sum):
    rows, rank = p_sum.shape
    return pl.pallas_call(
        orthonormal_body,
        out_shape=jax.ShapeDtypeStruct((rows, rank), jnp.bfloat16),
        in_specs=[pl.BlockSpec(memory_space=pltpu.VMEM)],
        out_specs=pl.BlockSpec(memory_space=pltpu.VMEM),
        cost_estimate=pl.CostEstimate(
            flops=4 * rows * rank * rank, bytes_accessed=6 * rows * rank, transcendentals=rank
        ),
        name="orthonormal",
    )(p_sum)


def shards(hidden_acts, out_grad, error_prev, right_prev):
    weight_grad = lax.dot_general(
        out_grad, hidden_acts, (((0,), (0,)), ((), ())), preferred_element_type=jnp.float32
    )
    compensated = (weight_grad + error_prev[0].astype(jnp.float32)).astype(jnp.bfloat16)
    partial_value = jnp.dot(compensated, right_prev, preferred_element_type=jnp.float32)
    rows = sum_at_owner(partial_value.astype(jnp.bfloat16), "replica")
    rows = rows.astype(jnp.float32).sum(axis=0)
    rows = copy_for_each(rows, "tensor").sum(axis=0)
    p_sum = collect(rows.astype(jnp.bfloat16), "replica")
    left_low = orthonormal(p_sum)
    share = lax.dot_general(
        compensated, left_low, (((0,), (0,)), ((), ())), preferred_element_type=jnp.float32
    )
    mine = sum_at_owner(share.astype(jnp.bfloat16), "replica").astype(jnp.float32).sum(axis=0)
    mine = mine / lax.axis_size("replica")
    right_low = collect(mine.astype(jnp.bfloat16), "replica")
    approx = lax.dot_general(
        left_low, right_low, (((1,), (1,)), ((), ())), preferred_element_type=jnp.float32
    )
    error_next = (compensated.astype(jnp.float32) - approx).astype(jnp.bfloat16)
    return (error_next[None], right_low.astype(jnp.float32))


def solution(mesh):
    return jax.shard_map(
        shards,
        mesh=mesh,
        in_specs=(
            P("replica", "tensor"),
            P("replica", None),
            P("replica", None, "tensor"),
            P("tensor", None),
        ),
        out_specs=(P("replica", None, "tensor"), P("tensor", None)),
        check_vma=False,
    )
```

```python
import jax
import jax.numpy as jnp
from jax import lax
from jax.experimental import pallas as pl
from jax.experimental.pallas import tpu as pltpu
from jax.sharding import PartitionSpec as P

EXACT = lax.Precision.HIGHEST
SUB, LANE = 8, 128
PIVOTS = 8
PANEL = 64


def sum_at_owner(value, axis):
    parts = lax.axis_size(axis)
    blocks = value.reshape(parts, value.shape[0] // parts, value.shape[1])
    return lax.all_to_all(blocks, axis, split_axis=0, concat_axis=0, tiled=True)


def copy_for_each(value, axis):
    copies = jnp.broadcast_to(value, (lax.axis_size(axis), *value.shape))
    return lax.all_to_all(copies, axis, split_axis=0, concat_axis=0, tiled=True)


def collect(value, axis):
    return copy_for_each(value, axis).reshape(-1, value.shape[1])


def eliminate(gram, right, base):
    height, width = gram.shape
    groups = height // SUB
    gram = gram.reshape(groups, SUB, width)
    right = right.reshape(groups, SUB, width)
    shape = (groups, SUB, width)
    row_index = lax.broadcasted_iota(jnp.int32, shape, 0) * SUB + lax.broadcasted_iota(
        jnp.int32, shape, 1
    )

    def row(value, i):
        return jnp.broadcast_to(value[i // SUB, i % SUB : i % SUB + 1, :], (SUB, width))

    pivots = []
    for first in range(0, height, PIVOTS):
        columns = [
            jnp.broadcast_to(gram[:, :, base + first + k : base + first + k + 1], shape)
            for k in range(PIVOTS)
        ]
        corner = {
            (i, k): row(columns[k], first + i) for k in range(PIVOTS) for i in range(k + 1)
        }
        gram_rows = [row(gram, first + i) for i in range(PIVOTS)]
        right_rows = [row(right, first + i) for i in range(PIVOTS)]
        factors = []
        for i in range(PIVOTS):
            inverse = 1.0 / corner[i, i]
            pivots.append(corner[i, i][:1])
            for k in range(i + 1, PIVOTS):
                ratio = corner[i, k] * inverse
                for j in range(k, PIVOTS):
                    corner[k, j] = corner[k, j] - ratio * corner[i, j]
                columns[k] = columns[k] - columns[i] * ratio
                gram_rows[k] = gram_rows[k] - gram_rows[i] * ratio
                right_rows[k] = right_rows[k] - right_rows[i] * ratio
            factors.append(jnp.where(row_index > first + i, columns[i] * inverse, 0.0))
        for i in range(PIVOTS):
            gram = gram - factors[i] * gram_rows[i]
            right = right - factors[i] * right_rows[i]
    scale = lax.rsqrt(jnp.concatenate(pivots, axis=0))
    return gram.reshape(height, width) * scale, right.reshape(height, width) * scale


def factor_body(p_ref, out_ref):
    p_sum = p_ref[...]
    gram = lax.dot_general(
        p_sum, p_sum, (((0,), (0,)), ((), ())), preferred_element_type=jnp.float32
    )
    rank = gram.shape[0]
    across = lax.broadcasted_iota(jnp.int32, (rank, rank), 0)
    along = lax.broadcasted_iota(jnp.int32, (rank, rank), 1)
    right = jnp.where(across == along, 1.0, 0.0)
    inverse = []
    for base in range(0, rank, PANEL):
        upper, done = eliminate(gram[:PANEL], right[:PANEL], base)
        inverse.append(done)
        if base + PANEL < rank:
            update = lax.dot_general(
                upper,
                jnp.concatenate([upper, done], axis=1),
                (((0,), (0,)), ((), ())),
                precision=EXACT,
                preferred_element_type=jnp.float32,
            )[base + PANEL :]
            gram = gram[PANEL:] - update[:, :rank]
            right = right[PANEL:] - update[:, rank:]
    inverse = jnp.concatenate(inverse, axis=0)
    high = inverse.astype(jnp.bfloat16)
    low = (inverse - high.astype(jnp.float32)).astype(jnp.bfloat16)
    across = (((1,), (1,)), ((), ()))
    left = lax.dot_general(p_sum, high, across, preferred_element_type=jnp.float32)
    left = left + lax.dot_general(p_sum, low, across, preferred_element_type=jnp.float32)
    rows = p_sum.shape[0]
    out_ref[:rows, :] = left.astype(jnp.bfloat16)
    out_ref[rows : rows + rank, :] = high
    out_ref[rows + rank :, :] = low


def inverse_factor(p_sum):
    rows, rank = p_sum.shape
    return pl.pallas_call(
        factor_body,
        out_shape=jax.ShapeDtypeStruct((rows + 2 * rank, rank), jnp.bfloat16),
        in_specs=[pl.BlockSpec(memory_space=pltpu.VMEM)],
        out_specs=pl.BlockSpec(memory_space=pltpu.VMEM),
        cost_estimate=pl.CostEstimate(
            flops=4 * rows * rank * rank, bytes_accessed=6 * rows * rank, transcendentals=rank
        ),
        name="inverse_factor",
    )(p_sum)


def shards(hidden_acts, out_grad, error_prev, right_prev):
    weight_grad = lax.dot_general(
        out_grad, hidden_acts, (((0,), (0,)), ((), ())), preferred_element_type=jnp.float32
    )
    compensated = (weight_grad + error_prev[0].astype(jnp.float32)).astype(jnp.bfloat16)
    partial_value = jnp.dot(compensated, right_prev, preferred_element_type=jnp.float32)
    rows = sum_at_owner(partial_value.astype(jnp.bfloat16), "replica")
    rows = rows.astype(jnp.float32).sum(axis=0)
    rows = copy_for_each(rows.astype(jnp.bfloat16), "tensor").astype(jnp.float32).sum(axis=0)
    p_sum = collect(rows.astype(jnp.bfloat16), "replica")
    rows, rank = p_sum.shape
    factors = inverse_factor(p_sum)
    left_low = factors[:rows]
    inverse = factors[rows : rows + rank].astype(jnp.float32) + factors[rows + rank :].astype(jnp.float32)
    scaled = inverse / lax.axis_size("replica")
    left_low, scaled = lax.optimization_barrier((left_low, scaled))
    share = lax.dot_general(
        compensated, p_sum, (((0,), (0,)), ((), ())), preferred_element_type=jnp.float32
    )
    mine = sum_at_owner(share.astype(jnp.bfloat16), "replica").astype(jnp.float32).sum(axis=0)
    mine = lax.dot_general(
        mine, scaled, (((1,), (1,)), ((), ())), precision=lax.Precision.HIGH, preferred_element_type=jnp.float32
    )
    right_low = collect(mine.astype(jnp.bfloat16), "replica")
    approx = lax.dot_general(
        left_low, right_low, (((1,), (1,)), ((), ())), preferred_element_type=jnp.float32
    )
    error_next = (compensated.astype(jnp.float32) - approx).astype(jnp.bfloat16)
    return (error_next[None], right_low.astype(jnp.float32))


def solution(mesh):
    return jax.shard_map(
        shards,
        mesh=mesh,
        in_specs=(
            P("replica", "tensor"),
            P("replica", None),
            P("replica", None, "tensor"),
            P("tensor", None),
        ),
        out_specs=(P("replica", None, "tensor"), P("tensor", None)),
        check_vma=False,
    )
```

```python
import jax
import jax.numpy as jnp
from jax import lax
from jax.experimental import pallas as pl
from jax.experimental.pallas import tpu as pltpu
from jax.sharding import PartitionSpec as P

EXACT = lax.Precision.HIGHEST
SUB, LANE = 8, 128
PIVOTS = 8
PANEL = 64
CHUNKS = 4


def sum_at_owner(value, axis):
    parts = lax.axis_size(axis)
    blocks = value.reshape(parts, value.shape[0] // parts, value.shape[1])
    return lax.all_to_all(blocks, axis, split_axis=0, concat_axis=0, tiled=True)


def copy_for_each(value, axis):
    copies = jnp.broadcast_to(value, (lax.axis_size(axis), *value.shape))
    return lax.all_to_all(copies, axis, split_axis=0, concat_axis=0, tiled=True)


def collect(value, axis):
    return copy_for_each(value, axis).reshape(-1, value.shape[1])


def eliminate(gram, right, base):
    height, width = gram.shape
    groups = height // SUB
    gram = gram.reshape(groups, SUB, width)
    right = right.reshape(groups, SUB, width)

    def row(value, i):
        return jnp.broadcast_to(value[i // SUB, i % SUB : i % SUB + 1, :], (SUB, width))

    pivots = []
    finished = []
    for first in range(0, height, PIVOTS):
        left = (height - first) // SUB
        shape = (left, SUB, width)
        row_index = lax.broadcasted_iota(jnp.int32, shape, 0) * SUB + lax.broadcasted_iota(
            jnp.int32, shape, 1
        )
        columns = [
            jnp.broadcast_to(gram[:, :, base + first + k : base + first + k + 1], shape)
            for k in range(PIVOTS)
        ]
        corner = {(i, k): row(columns[k], i) for k in range(PIVOTS) for i in range(k + 1)}
        gram_rows = [row(gram, i) for i in range(PIVOTS)]
        right_rows = [row(right, i) for i in range(PIVOTS)]
        factors = []
        for i in range(PIVOTS):
            inverse = 1.0 / corner[i, i]
            pivots.append(corner[i, i][:1])
            for k in range(i + 1, PIVOTS):
                ratio = corner[i, k] * inverse
                for j in range(k, PIVOTS):
                    corner[k, j] = corner[k, j] - ratio * corner[i, j]
                columns[k] = columns[k] - columns[i] * ratio
                gram_rows[k] = gram_rows[k] - gram_rows[i] * ratio
                right_rows[k] = right_rows[k] - right_rows[i] * ratio
            factors.append(jnp.where(row_index > i, columns[i] * inverse, 0.0))
        for i in range(PIVOTS):
            gram = gram - factors[i] * gram_rows[i]
            right = right - factors[i] * right_rows[i]
        finished.append((gram[: PIVOTS // SUB], right[: PIVOTS // SUB]))
        gram, right = gram[PIVOTS // SUB :], right[PIVOTS // SUB :]
    scale = lax.rsqrt(jnp.concatenate(pivots, axis=0))
    gram, right = (jnp.concatenate(parts, axis=0) for parts in zip(*finished, strict=True))
    return gram.reshape(height, width) * scale, right.reshape(height, width) * scale


def factor_body(p_ref, out_ref):
    p_sum = p_ref[...]
    gram = lax.dot_general(
        p_sum, p_sum, (((0,), (0,)), ((), ())), preferred_element_type=jnp.float32
    )
    rank = gram.shape[0]
    across = lax.broadcasted_iota(jnp.int32, (rank, rank), 0)
    along = lax.broadcasted_iota(jnp.int32, (rank, rank), 1)
    right = jnp.where(across == along, 1.0, 0.0)
    inverse = []
    for base in range(0, rank, PANEL):
        upper, done = eliminate(gram[:PANEL], right[:PANEL], base)
        inverse.append(done)
        if base + PANEL < rank:
            update = lax.dot_general(
                upper,
                jnp.concatenate([upper, done], axis=1),
                (((0,), (0,)), ((), ())),
                precision=EXACT,
                preferred_element_type=jnp.float32,
            )[base + PANEL :]
            gram = gram[PANEL:] - update[:, :rank]
            right = right[PANEL:] - update[:, rank:]
    inverse = jnp.concatenate(inverse, axis=0)
    high = inverse.astype(jnp.bfloat16)
    low = (inverse - high.astype(jnp.float32)).astype(jnp.bfloat16)
    across = (((1,), (1,)), ((), ()))
    left = lax.dot_general(p_sum, high, across, preferred_element_type=jnp.float32)
    left = left + lax.dot_general(p_sum, low, across, preferred_element_type=jnp.float32)
    rows = p_sum.shape[0]
    out_ref[:rows, :] = left.astype(jnp.bfloat16)
    out_ref[rows : rows + rank, :] = high
    out_ref[rows + rank :, :] = low


def inverse_factor(p_sum):
    rows, rank = p_sum.shape
    return pl.pallas_call(
        factor_body,
        out_shape=jax.ShapeDtypeStruct((rows + 2 * rank, rank), jnp.bfloat16),
        in_specs=[pl.BlockSpec(memory_space=pltpu.VMEM)],
        out_specs=pl.BlockSpec(memory_space=pltpu.VMEM),
        cost_estimate=pl.CostEstimate(
            flops=4 * rows * rank * rank, bytes_accessed=6 * rows * rank, transcendentals=rank
        ),
        compiler_params=pltpu.CompilerParams(vmem_limit_bytes=8 * 1024 * 1024),
        name="inverse_factor",
    )(p_sum)


def outputs_body(left_ref, right_ref, value_ref, error_ref, next_ref, error, wide, done):
    right = right_ref[...]
    wide[...] = right.astype(jnp.float32)
    copies = [pltpu.make_async_copy(wide, next_ref, done.at[CHUNKS])]
    copies[0].start()
    rows = value_ref.shape[0] // CHUNKS
    for i in range(CHUNKS):
        own = pl.ds(i * rows, rows)
        approx = lax.dot_general(
            left_ref[own, :], right, (((1,), (1,)), ((), ())), preferred_element_type=jnp.float32
        )
        error[own, :] = (value_ref[own, :].astype(jnp.float32) - approx).astype(error.dtype)
        copies.append(pltpu.make_async_copy(error.at[own], error_ref.at[0, own], done.at[i]))
        copies[-1].start()
    for copy in copies:
        copy.wait()


def outputs(left_low, right_low, compensated):
    (rows, width), (_, rank) = compensated.shape, right_low.shape
    return pl.pallas_call(
        outputs_body,
        out_shape=(
            jax.ShapeDtypeStruct((1, rows, width), jnp.bfloat16),
            jax.ShapeDtypeStruct((width, rank), jnp.float32),
        ),
        in_specs=[pl.BlockSpec(memory_space=pltpu.VMEM)] * 3,
        out_specs=(pl.BlockSpec(memory_space=pl.ANY),) * 2,
        scratch_shapes=[
            pltpu.VMEM((rows, width), jnp.bfloat16),
            pltpu.VMEM((width, rank), jnp.float32),
            pltpu.SemaphoreType.DMA((CHUNKS + 1,)),
        ],
        cost_estimate=pl.CostEstimate(
            flops=2 * rows * width * rank,
            bytes_accessed=4 * rows * width + 4 * width * rank,
            transcendentals=0,
        ),
        compiler_params=pltpu.CompilerParams(vmem_limit_bytes=16 * 1024 * 1024),
        name="outputs",
    )(left_low, right_low, compensated)


def shards(hidden_acts, out_grad, error_prev, right_prev):
    weight_grad = lax.dot_general(
        out_grad, hidden_acts, (((0,), (0,)), ((), ())), preferred_element_type=jnp.float32
    )
    compensated = (weight_grad + error_prev[0].astype(jnp.float32)).astype(jnp.bfloat16)
    partial_value = jnp.dot(compensated, right_prev, preferred_element_type=jnp.float32)
    rows = sum_at_owner(partial_value.astype(jnp.bfloat16), "replica")
    rows = rows.astype(jnp.float32).sum(axis=0)
    rows = copy_for_each(rows.astype(jnp.bfloat16), "tensor").astype(jnp.float32).sum(axis=0)
    p_sum = collect(rows.astype(jnp.bfloat16), "replica")
    rows, rank = p_sum.shape
    factors = inverse_factor(p_sum)
    left_low = factors[:rows]
    inverse = factors[rows : rows + rank].astype(jnp.float32) + factors[rows + rank :].astype(jnp.float32)
    scaled = inverse / lax.axis_size("replica")
    left_low, scaled = lax.optimization_barrier((left_low, scaled))
    share = lax.dot_general(
        compensated, p_sum, (((0,), (0,)), ((), ())), preferred_element_type=jnp.float32
    )
    mine = sum_at_owner(share.astype(jnp.bfloat16), "replica").astype(jnp.float32).sum(axis=0)
    mine = lax.dot_general(
        mine, scaled, (((1,), (1,)), ((), ())), precision=lax.Precision.HIGH, preferred_element_type=jnp.float32
    )
    right_low = collect(mine.astype(jnp.bfloat16), "replica")
    return outputs(left_low, right_low, compensated)


def solution(mesh):
    return jax.shard_map(
        shards,
        mesh=mesh,
        in_specs=(
            P("replica", "tensor"),
            P("replica", None),
            P("replica", None, "tensor"),
            P("tensor", None),
        ),
        out_specs=(P("replica", None, "tensor"), P("tensor", None)),
        check_vma=False,
    )
```

```python
import jax
import jax.numpy as jnp
from jax import lax
from jax.experimental import pallas as pl
from jax.experimental.pallas import tpu as pltpu
from jax.sharding import PartitionSpec as P

EXACT = lax.Precision.HIGHEST
SUB, LANE = 8, 128
PIVOTS = 8
PANEL = 64
CHUNKS = 4
PIECES = 3


def sum_at_owner(value, axis):
    parts = lax.axis_size(axis)
    blocks = value.reshape(parts, value.shape[0] // parts, value.shape[1])
    return lax.all_to_all(blocks, axis, split_axis=0, concat_axis=0, tiled=True)


def copy_for_each(value, axis):
    copies = jnp.broadcast_to(value, (lax.axis_size(axis), *value.shape))
    return lax.all_to_all(copies, axis, split_axis=0, concat_axis=0, tiled=True)


def collect(value, axis):
    return copy_for_each(value, axis).reshape(-1, value.shape[1])


def eliminate(gram, right, base):
    height, width = gram.shape
    groups = height // SUB
    gram = gram.reshape(groups, SUB, width)
    right = right.reshape(groups, SUB, width)

    def row(value, i):
        return jnp.broadcast_to(value[i // SUB, i % SUB : i % SUB + 1, :], (SUB, width))

    pivots = []
    finished = []
    for first in range(0, height, PIVOTS):
        left = (height - first) // SUB
        shape = (left, SUB, width)
        row_index = lax.broadcasted_iota(jnp.int32, shape, 0) * SUB + lax.broadcasted_iota(
            jnp.int32, shape, 1
        )
        columns = [
            jnp.broadcast_to(gram[:, :, base + first + k : base + first + k + 1], shape)
            for k in range(PIVOTS)
        ]
        corner = {(i, k): row(columns[k], i) for k in range(PIVOTS) for i in range(k + 1)}
        gram_rows = [row(gram, i) for i in range(PIVOTS)]
        right_rows = [row(right, i) for i in range(PIVOTS)]
        factors = []
        for i in range(PIVOTS):
            inverse = 1.0 / corner[i, i]
            pivots.append(corner[i, i][:1])
            for k in range(i + 1, PIVOTS):
                ratio = corner[i, k] * inverse
                for j in range(k, PIVOTS):
                    corner[k, j] = corner[k, j] - ratio * corner[i, j]
                columns[k] = columns[k] - columns[i] * ratio
                gram_rows[k] = gram_rows[k] - gram_rows[i] * ratio
                right_rows[k] = right_rows[k] - right_rows[i] * ratio
            factors.append(jnp.where(row_index > i, columns[i] * inverse, 0.0))
        for i in range(PIVOTS):
            gram = gram - factors[i] * gram_rows[i]
            right = right - factors[i] * right_rows[i]
        finished.append((gram[: PIVOTS // SUB], right[: PIVOTS // SUB]))
        gram, right = gram[PIVOTS // SUB :], right[PIVOTS // SUB :]
    scale = lax.rsqrt(jnp.concatenate(pivots, axis=0))
    gram, right = (jnp.concatenate(parts, axis=0) for parts in zip(*finished, strict=True))
    return gram.reshape(height, width) * scale, right.reshape(height, width) * scale


def factor_body(p_ref, out_ref):
    p_sum = p_ref[...]
    gram = lax.dot_general(
        p_sum, p_sum, (((0,), (0,)), ((), ())), preferred_element_type=jnp.float32
    )
    rank = gram.shape[0]
    across = lax.broadcasted_iota(jnp.int32, (rank, rank), 0)
    along = lax.broadcasted_iota(jnp.int32, (rank, rank), 1)
    right = jnp.where(across == along, 1.0, 0.0)
    inverse = []
    for base in range(0, rank, PANEL):
        upper, done = eliminate(gram[:PANEL], right[:PANEL], base)
        inverse.append(done)
        if base + PANEL < rank:
            update = lax.dot_general(
                upper,
                jnp.concatenate([upper, done], axis=1),
                (((0,), (0,)), ((), ())),
                precision=EXACT,
                preferred_element_type=jnp.float32,
            )[base + PANEL :]
            gram = gram[PANEL:] - update[:, :rank]
            right = right[PANEL:] - update[:, rank:]
    inverse = jnp.concatenate(inverse, axis=0)
    high = inverse.astype(jnp.bfloat16)
    low = (inverse - high.astype(jnp.float32)).astype(jnp.bfloat16)
    across = (((1,), (1,)), ((), ()))
    left = lax.dot_general(p_sum, high, across, preferred_element_type=jnp.float32)
    left = left + lax.dot_general(p_sum, low, across, preferred_element_type=jnp.float32)
    rows = p_sum.shape[0]
    out_ref[:rows, :] = left.astype(jnp.bfloat16)
    out_ref[rows : rows + rank, :] = high
    out_ref[rows + rank :, :] = low


def inverse_factor(p_sum):
    rows, rank = p_sum.shape
    return pl.pallas_call(
        factor_body,
        out_shape=jax.ShapeDtypeStruct((rows + 2 * rank, rank), jnp.bfloat16),
        in_specs=[pl.BlockSpec(memory_space=pltpu.VMEM)],
        out_specs=pl.BlockSpec(memory_space=pltpu.VMEM),
        cost_estimate=pl.CostEstimate(
            flops=4 * rows * rank * rank, bytes_accessed=6 * rows * rank, transcendentals=rank
        ),
        compiler_params=pltpu.CompilerParams(vmem_limit_bytes=8 * 1024 * 1024),
        name="inverse_factor",
    )(p_sum)


def compensate_body(
    grad_hbm, acts_hbm, error_hbm, right_hbm, value_ref, part_ref, grad, acts, error, right, done
):
    rows = value_ref.shape[0] // PIECES
    pieces = [pl.ds(i * rows, rows) for i in range(PIECES)]
    grad_copy = pltpu.make_async_copy(grad_hbm, grad, done.at[PIECES])
    acts_copy = pltpu.make_async_copy(acts_hbm, acts, done.at[PIECES + 1])
    right_copy = pltpu.make_async_copy(right_hbm, right, done.at[PIECES + 2])
    error_copies = [
        pltpu.make_async_copy(error_hbm.at[0, own], error.at[own], done.at[i])
        for i, own in enumerate(pieces)
    ]
    grad_copy.start()
    acts_copy.start()
    error_copies[0].start()
    right_copy.start()
    for copy in error_copies[1:]:
        copy.start()
    grad_copy.wait()
    acts_copy.wait()
    for i, own in enumerate(pieces):
        weight_grad = lax.dot_general(
            grad[:, own], acts[...], (((0,), (0,)), ((), ())), preferred_element_type=jnp.float32
        )
        error_copies[i].wait()
        value = (weight_grad + error[own, :].astype(jnp.float32)).astype(value_ref.dtype)
        value_ref[own, :] = value
        if i == 0:
            right_copy.wait()
        part_ref[own, :] = jnp.dot(
            value, right[...], preferred_element_type=jnp.float32
        ).astype(part_ref.dtype)


def compensate(hidden_acts, out_grad, error_prev, right_prev):
    (tokens, rows), width, rank = out_grad.shape, hidden_acts.shape[1], right_prev.shape[1]
    values = (out_grad, hidden_acts, error_prev, right_prev)
    return pl.pallas_call(
        compensate_body,
        out_shape=(
            jax.ShapeDtypeStruct((rows, width), jnp.bfloat16),
            jax.ShapeDtypeStruct((rows, rank), jnp.bfloat16),
        ),
        in_specs=[pl.BlockSpec(memory_space=pl.ANY)] * 4,
        out_specs=(pl.BlockSpec(memory_space=pltpu.VMEM),) * 2,
        scratch_shapes=[
            pltpu.VMEM((tokens, rows), jnp.bfloat16),
            pltpu.VMEM((tokens, width), jnp.bfloat16),
            pltpu.VMEM((rows, width), jnp.bfloat16),
            pltpu.VMEM((width, rank), jnp.bfloat16),
            pltpu.SemaphoreType.DMA((PIECES + 3,)),
        ],
        compiler_params=pltpu.CompilerParams(vmem_limit_bytes=16 * 1024 * 1024),
        name="compensate",
    )(*(pltpu.with_memory_space_constraint(value, pltpu.HBM) for value in values))


def product_body(value_ref, p_ref, share_ref, share, done):
    p_rows = p_ref[...].T
    width = value_ref.shape[1] // CHUNKS
    copies = []
    for i in range(CHUNKS):
        own = pl.ds(i * width, width)
        part = jnp.dot(p_rows, value_ref[:, own], preferred_element_type=jnp.float32)
        share[own, :] = part.T.astype(share.dtype)
        copies.append(pltpu.make_async_copy(share.at[own], share_ref.at[own], done.at[i]))
        copies[-1].start()
    for copy in copies:
        copy.wait()


def product(compensated, p_sum):
    (rows, width), (_, rank) = compensated.shape, p_sum.shape
    return pl.pallas_call(
        product_body,
        out_shape=jax.ShapeDtypeStruct((width, rank), jnp.bfloat16),
        in_specs=[pl.BlockSpec(memory_space=pltpu.VMEM)] * 2,
        out_specs=pl.BlockSpec(memory_space=pl.ANY),
        scratch_shapes=[
            pltpu.VMEM((width, rank), jnp.bfloat16),
            pltpu.SemaphoreType.DMA((CHUNKS,)),
        ],
        cost_estimate=pl.CostEstimate(
            flops=2 * rows * width * rank,
            bytes_accessed=2 * (rows * width + rows * rank + width * rank),
            transcendentals=0,
        ),
        compiler_params=pltpu.CompilerParams(vmem_limit_bytes=16 * 1024 * 1024),
        name="product",
    )(compensated, p_sum)


def outputs_body(left_ref, right_ref, value_ref, error_ref, next_ref, error, wide, done):
    right = right_ref[...]
    wide[...] = right.astype(jnp.float32)
    copies = [pltpu.make_async_copy(wide, next_ref, done.at[CHUNKS])]
    copies[0].start()
    rows = value_ref.shape[0] // CHUNKS
    for i in range(CHUNKS):
        own = pl.ds(i * rows, rows)
        approx = lax.dot_general(
            left_ref[own, :], right, (((1,), (1,)), ((), ())), preferred_element_type=jnp.float32
        )
        error[own, :] = (value_ref[own, :].astype(jnp.float32) - approx).astype(error.dtype)
        copies.append(pltpu.make_async_copy(error.at[own], error_ref.at[0, own], done.at[i]))
        copies[-1].start()
    for copy in copies:
        copy.wait()


def outputs(left_low, right_low, compensated):
    (rows, width), (_, rank) = compensated.shape, right_low.shape
    return pl.pallas_call(
        outputs_body,
        out_shape=(
            jax.ShapeDtypeStruct((1, rows, width), jnp.bfloat16),
            jax.ShapeDtypeStruct((width, rank), jnp.float32),
        ),
        in_specs=[pl.BlockSpec(memory_space=pltpu.VMEM)] * 3,
        out_specs=(pl.BlockSpec(memory_space=pl.ANY),) * 2,
        scratch_shapes=[
            pltpu.VMEM((rows, width), jnp.bfloat16),
            pltpu.VMEM((width, rank), jnp.float32),
            pltpu.SemaphoreType.DMA((CHUNKS + 1,)),
        ],
        cost_estimate=pl.CostEstimate(
            flops=2 * rows * width * rank,
            bytes_accessed=4 * rows * width + 4 * width * rank,
            transcendentals=0,
        ),
        compiler_params=pltpu.CompilerParams(vmem_limit_bytes=16 * 1024 * 1024),
        name="outputs",
    )(left_low, right_low, compensated)


def shards(hidden_acts, out_grad, error_prev, right_prev):
    compensated, partial_value = compensate(hidden_acts, out_grad, error_prev, right_prev)
    rows = sum_at_owner(partial_value, "replica")
    rows = rows.astype(jnp.float32).sum(axis=0)
    rows = copy_for_each(rows.astype(jnp.bfloat16), "tensor").astype(jnp.float32).sum(axis=0)
    p_sum = collect(rows.astype(jnp.bfloat16), "replica")
    rows, rank = p_sum.shape
    factors = inverse_factor(p_sum)
    left_low = factors[:rows]
    inverse = factors[rows : rows + rank].astype(jnp.float32) + factors[rows + rank :].astype(jnp.float32)
    scaled = inverse / lax.axis_size("replica")
    left_low, scaled = lax.optimization_barrier((left_low, scaled))
    share = product(compensated, p_sum)
    mine = sum_at_owner(share, "replica").astype(jnp.float32).sum(axis=0)
    mine = lax.dot_general(
        mine, scaled, (((1,), (1,)), ((), ())), precision=lax.Precision.HIGH, preferred_element_type=jnp.float32
    )
    right_low = collect(mine.astype(jnp.bfloat16), "replica")
    return outputs(left_low, right_low, compensated)


def solution(mesh):
    return jax.shard_map(
        shards,
        mesh=mesh,
        in_specs=(
            P("replica", "tensor"),
            P("replica", None),
            P("replica", None, "tensor"),
            P("tensor", None),
        ),
        out_specs=(P("replica", None, "tensor"), P("tensor", None)),
        check_vma=False,
    )
```

```python
import jax
import jax.numpy as jnp
from jax import lax
from jax.experimental import pallas as pl
from jax.experimental.pallas import tpu as pltpu
from jax.sharding import PartitionSpec as P

EXACT = lax.Precision.HIGHEST
SUB, LANE = 8, 128
PIVOTS = 8
PANEL = 64
CHUNKS = 4
PIECES = 3


def sum_at_owner(value, axis):
    parts = lax.axis_size(axis)
    blocks = value.reshape(parts, value.shape[0] // parts, value.shape[1])
    return lax.all_to_all(blocks, axis, split_axis=0, concat_axis=0, tiled=True)


def copy_for_each(value, axis):
    copies = jnp.broadcast_to(value, (lax.axis_size(axis), *value.shape))
    return lax.all_to_all(copies, axis, split_axis=0, concat_axis=0, tiled=True)


def collect(value, axis):
    return copy_for_each(value, axis).reshape(-1, value.shape[1])


def eliminate(gram, right, base):
    height, width = gram.shape
    groups = height // SUB
    gram = gram.reshape(groups, SUB, width)
    right = right.reshape(groups, SUB, width)

    def row(value, i):
        return jnp.broadcast_to(value[i // SUB, i % SUB : i % SUB + 1, :], (SUB, width))

    pivots = []
    finished = []
    for first in range(0, height, PIVOTS):
        left = (height - first) // SUB
        shape = (left, SUB, width)
        row_index = lax.broadcasted_iota(jnp.int32, shape, 0) * SUB + lax.broadcasted_iota(
            jnp.int32, shape, 1
        )
        columns = [
            jnp.broadcast_to(gram[:, :, base + first + k : base + first + k + 1], shape)
            for k in range(PIVOTS)
        ]
        corner = {(i, k): row(columns[k], i) for k in range(PIVOTS) for i in range(k + 1)}
        gram_rows = [row(gram, i) for i in range(PIVOTS)]
        right_rows = [row(right, i) for i in range(PIVOTS)]
        factors = []
        for i in range(PIVOTS):
            inverse = 1.0 / corner[i, i]
            pivots.append(corner[i, i][:1])
            for k in range(i + 1, PIVOTS):
                ratio = corner[i, k] * inverse
                for j in range(k, PIVOTS):
                    corner[k, j] = corner[k, j] - ratio * corner[i, j]
                columns[k] = columns[k] - columns[i] * ratio
                gram_rows[k] = gram_rows[k] - gram_rows[i] * ratio
                right_rows[k] = right_rows[k] - right_rows[i] * ratio
            factors.append(jnp.where(row_index > i, columns[i] * inverse, 0.0))
        for i in range(PIVOTS):
            gram = gram - factors[i] * gram_rows[i]
            right = right - factors[i] * right_rows[i]
        finished.append((gram[: PIVOTS // SUB], right[: PIVOTS // SUB]))
        gram, right = gram[PIVOTS // SUB :], right[PIVOTS // SUB :]
    scale = lax.rsqrt(jnp.concatenate(pivots, axis=0))
    gram, right = (jnp.concatenate(parts, axis=0) for parts in zip(*finished, strict=True))
    return gram.reshape(height, width) * scale, right.reshape(height, width) * scale


def factor_body(p_ref, out_ref):
    p_sum = p_ref[...]
    gram = lax.dot_general(
        p_sum, p_sum, (((0,), (0,)), ((), ())), preferred_element_type=jnp.float32
    )
    rank = gram.shape[0]
    across = lax.broadcasted_iota(jnp.int32, (rank, rank), 0)
    along = lax.broadcasted_iota(jnp.int32, (rank, rank), 1)
    right = jnp.where(across == along, 1.0, 0.0)
    inverse = []
    for base in range(0, rank, PANEL):
        upper, done = eliminate(gram[:PANEL], right[:PANEL], base)
        inverse.append(done)
        if base + PANEL < rank:
            update = lax.dot_general(
                upper,
                jnp.concatenate([upper, done], axis=1),
                (((0,), (0,)), ((), ())),
                precision=EXACT,
                preferred_element_type=jnp.float32,
            )[base + PANEL :]
            gram = gram[PANEL:] - update[:, :rank]
            right = right[PANEL:] - update[:, rank:]
    inverse = jnp.concatenate(inverse, axis=0)
    high = inverse.astype(jnp.bfloat16)
    low = (inverse - high.astype(jnp.float32)).astype(jnp.bfloat16)
    across = (((1,), (1,)), ((), ()))
    left = lax.dot_general(p_sum, high, across, preferred_element_type=jnp.float32)
    left = left + lax.dot_general(p_sum, low, across, preferred_element_type=jnp.float32)
    rows = p_sum.shape[0]
    out_ref[:rows, :] = left.astype(jnp.bfloat16)
    out_ref[rows : rows + rank, :] = high
    out_ref[rows + rank :, :] = low


def inverse_factor(p_sum):
    rows, rank = p_sum.shape
    return pl.pallas_call(
        factor_body,
        out_shape=jax.ShapeDtypeStruct((rows + 2 * rank, rank), jnp.bfloat16),
        in_specs=[pl.BlockSpec(memory_space=pltpu.VMEM)],
        out_specs=pl.BlockSpec(memory_space=pltpu.VMEM),
        cost_estimate=pl.CostEstimate(
            flops=4 * rows * rank * rank, bytes_accessed=6 * rows * rank, transcendentals=rank
        ),
        compiler_params=pltpu.CompilerParams(vmem_limit_bytes=8 * 1024 * 1024),
        name="inverse_factor",
    )(p_sum)


def compensate_body(
    grad_hbm, acts_hbm, error_hbm, right_hbm, value_ref, part_ref, grad, acts, error, right, done
):
    rows = value_ref.shape[0] // PIECES
    pieces = [pl.ds(i * rows, rows) for i in range(PIECES)]
    half = acts.shape[0] // 2
    halves = [pl.ds(0, half), pl.ds(half, half)]
    factor_copies = [
        [
            pltpu.make_async_copy(source.at[own], target.at[own], done.at[PIECES + 1 + 2 * i + j])
            for j, (source, target) in enumerate(((grad_hbm, grad), (acts_hbm, acts)))
        ]
        for i, own in enumerate(halves)
    ]
    right_copy = pltpu.make_async_copy(right_hbm, right, done.at[PIECES])
    error_copies = [
        pltpu.make_async_copy(error_hbm.at[0, own], error.at[own], done.at[i])
        for i, own in enumerate(pieces)
    ]
    for copies in factor_copies:
        for copy in copies:
            copy.start()
    error_copies[0].start()
    right_copy.start()
    for copy in error_copies[1:]:
        copy.start()
    for i, own in enumerate(pieces):
        weight_grad = 0.0
        for copies, tokens in zip(factor_copies, halves, strict=True):
            if i == 0:
                for copy in copies:
                    copy.wait()
            weight_grad += lax.dot_general(
                grad[tokens, own],
                acts[tokens, :],
                (((0,), (0,)), ((), ())),
                preferred_element_type=jnp.float32,
            )
        error_copies[i].wait()
        value = (weight_grad + error[own, :].astype(jnp.float32)).astype(value_ref.dtype)
        value_ref[own, :] = value
        if i == 0:
            right_copy.wait()
        part_ref[own, :] = jnp.dot(
            value, right[...], preferred_element_type=jnp.float32
        ).astype(part_ref.dtype)


def compensate(hidden_acts, out_grad, error_prev, right_prev):
    (tokens, rows), width, rank = out_grad.shape, hidden_acts.shape[1], right_prev.shape[1]
    values = (out_grad, hidden_acts, error_prev, right_prev)
    return pl.pallas_call(
        compensate_body,
        out_shape=(
            jax.ShapeDtypeStruct((rows, width), jnp.bfloat16),
            jax.ShapeDtypeStruct((rows, rank), jnp.bfloat16),
        ),
        in_specs=[pl.BlockSpec(memory_space=pl.ANY)] * 4,
        out_specs=(pl.BlockSpec(memory_space=pltpu.VMEM),) * 2,
        scratch_shapes=[
            pltpu.VMEM((tokens, rows), jnp.bfloat16),
            pltpu.VMEM((tokens, width), jnp.bfloat16),
            pltpu.VMEM((rows, width), jnp.bfloat16),
            pltpu.VMEM((width, rank), jnp.bfloat16),
            pltpu.SemaphoreType.DMA((PIECES + 5,)),
        ],
        compiler_params=pltpu.CompilerParams(vmem_limit_bytes=16 * 1024 * 1024),
        name="compensate",
    )(*(pltpu.with_memory_space_constraint(value, pltpu.HBM) for value in values))


def product_body(value_ref, p_ref, share_ref, share, done):
    p_rows = p_ref[...].T
    width = value_ref.shape[1] // CHUNKS
    copies = []
    for i in range(CHUNKS):
        own = pl.ds(i * width, width)
        part = jnp.dot(p_rows, value_ref[:, own], preferred_element_type=jnp.float32)
        share[own, :] = part.T.astype(share.dtype)
        copies.append(pltpu.make_async_copy(share.at[own], share_ref.at[own], done.at[i]))
        copies[-1].start()
    for copy in copies:
        copy.wait()


def product(compensated, p_sum):
    (rows, width), (_, rank) = compensated.shape, p_sum.shape
    return pl.pallas_call(
        product_body,
        out_shape=jax.ShapeDtypeStruct((width, rank), jnp.bfloat16),
        in_specs=[pl.BlockSpec(memory_space=pltpu.VMEM)] * 2,
        out_specs=pl.BlockSpec(memory_space=pl.ANY),
        scratch_shapes=[
            pltpu.VMEM((width, rank), jnp.bfloat16),
            pltpu.SemaphoreType.DMA((CHUNKS,)),
        ],
        cost_estimate=pl.CostEstimate(
            flops=2 * rows * width * rank,
            bytes_accessed=2 * (rows * width + rows * rank + width * rank),
            transcendentals=0,
        ),
        compiler_params=pltpu.CompilerParams(vmem_limit_bytes=16 * 1024 * 1024),
        name="product",
    )(compensated, p_sum)


def outputs_body(left_ref, right_ref, value_ref, error_ref, next_ref, error, wide, done):
    right = right_ref[...]
    wide[...] = right.astype(jnp.float32)
    copies = [pltpu.make_async_copy(wide, next_ref, done.at[CHUNKS])]
    copies[0].start()
    rows = value_ref.shape[0] // CHUNKS
    for i in range(CHUNKS):
        own = pl.ds(i * rows, rows)
        approx = lax.dot_general(
            left_ref[own, :], right, (((1,), (1,)), ((), ())), preferred_element_type=jnp.float32
        )
        error[own, :] = (value_ref[own, :].astype(jnp.float32) - approx).astype(error.dtype)
        copies.append(pltpu.make_async_copy(error.at[own], error_ref.at[0, own], done.at[i]))
        copies[-1].start()
    for copy in copies:
        copy.wait()


def outputs(left_low, right_low, compensated):
    (rows, width), (_, rank) = compensated.shape, right_low.shape
    return pl.pallas_call(
        outputs_body,
        out_shape=(
            jax.ShapeDtypeStruct((1, rows, width), jnp.bfloat16),
            jax.ShapeDtypeStruct((width, rank), jnp.float32),
        ),
        in_specs=[pl.BlockSpec(memory_space=pltpu.VMEM)] * 3,
        out_specs=(pl.BlockSpec(memory_space=pl.ANY),) * 2,
        scratch_shapes=[
            pltpu.VMEM((rows, width), jnp.bfloat16),
            pltpu.VMEM((width, rank), jnp.float32),
            pltpu.SemaphoreType.DMA((CHUNKS + 1,)),
        ],
        cost_estimate=pl.CostEstimate(
            flops=2 * rows * width * rank,
            bytes_accessed=4 * rows * width + 4 * width * rank,
            transcendentals=0,
        ),
        compiler_params=pltpu.CompilerParams(vmem_limit_bytes=16 * 1024 * 1024),
        name="outputs",
    )(left_low, right_low, compensated)


def shards(hidden_acts, out_grad, error_prev, right_prev):
    compensated, partial_value = compensate(hidden_acts, out_grad, error_prev, right_prev)
    rows = sum_at_owner(partial_value, "replica")
    rows = rows.astype(jnp.float32).sum(axis=0)
    rows = copy_for_each(rows.astype(jnp.bfloat16), "tensor").astype(jnp.float32).sum(axis=0)
    p_sum = collect(rows.astype(jnp.bfloat16), "replica")
    rows, rank = p_sum.shape
    factors = inverse_factor(p_sum)
    left_low = factors[:rows]
    inverse = factors[rows : rows + rank].astype(jnp.float32) + factors[rows + rank :].astype(jnp.float32)
    scaled = inverse / lax.axis_size("replica")
    left_low, scaled = lax.optimization_barrier((left_low, scaled))
    share = product(compensated, p_sum)
    mine = sum_at_owner(share, "replica").astype(jnp.float32).sum(axis=0)
    mine = lax.dot_general(
        mine, scaled, (((1,), (1,)), ((), ())), precision=lax.Precision.HIGH, preferred_element_type=jnp.float32
    )
    right_low = collect(mine.astype(jnp.bfloat16), "replica")
    return outputs(left_low, right_low, compensated)


def solution(mesh):
    return jax.shard_map(
        shards,
        mesh=mesh,
        in_specs=(
            P("replica", "tensor"),
            P("replica", None),
            P("replica", None, "tensor"),
            P("tensor", None),
        ),
        out_specs=(P("replica", None, "tensor"), P("tensor", None)),
        check_vma=False,
    )
```
